768 devices in a mesh: energy: 12 (over z), elem: 32 (over y, x), space: 2 (over core).
Axes of the slice: x: 4, y: 8, z: 12, core: 2. Of those that a mesh axis runs over, the one named last changes fastest.
Arguments:
- cell_blocks: float32 [4, 256, 256], P('space'), may hold values from -4 to 23, as said below
- coupling_blocks: float32 [4, 256, 256], P('space'), may hold values from -1 to 5
- sigma_prev: bfloat16 [384, 4, 256, 256], P(('energy', 'elem'), 'space'), may hold values from -1 to 3, as said below
- shifts: int32 [4], replicated, may hold values from 1 to 32, as said below
- strengths: float32 [4], replicated, may hold values from 0.5 to 2
Outputs:
- sigma_next: float32 [384, 4, 256, 256], P('energy', 'space', 'elem')
The draws below stay inside these ranges and needn't reach their ends.
Inputs may be any that keep to these rules, and one draw needn't show every extreme that they name: `cell_blocks`: each block is symmetric. `sigma_prev`: each block is symmetric; every M and every X(i) of the steps is positive definite. `shifts`: one branch's offset equals 32.
All inputs are finite; a program needn't handle non-finite values.
Results may differ from the reference program's by a relative error of at most 0.0003.
Values sent between devices are 32-bit elements; how exact they have to be, the bound alone decides.
No kernel may reach another device: no remote copies, remote signals or barrier semaphores. Data moves between devices by JAX's collectives and lax.ppermute only.
A program may use at most 32 MiB of HBM per device.

```python
import math
import jax
import jax.numpy as jnp
from jax import lax

NORB = 256
MODES = 4
BLOCKS = 4
ENERGIES = 384
SMAX = 32


def draw_cell_blocks(key, part):
    split_keys = jax.random.split(key)
    jitter = jax.random.truncated_normal(split_keys[0], -3.0, 3.0, (BLOCKS, NORB, NORB), jnp.float32)
    onsite = jax.random.uniform(split_keys[1], (BLOCKS, NORB), jnp.float32, 17.5, 18.5)
    spread_scale = 2.5 / math.sqrt(NORB)
    mirrored = (jitter + jnp.swapaxes(jitter, 1, 2)) * spread_scale
    return mirrored + onsite[:, :, None] * jnp.eye(NORB, dtype=jnp.float32)


def draw_coupling_blocks(key, part):
    split_keys = jax.random.split(key, 3)
    block_keys = jax.random.split(split_keys[0], BLOCKS)
    orders = jax.vmap(lambda block_key: jax.random.permutation(block_key, NORB))(block_keys)
    partner = (orders[:, :, None] == jnp.arange(NORB)[None, None, :]).astype(jnp.float32)
    magnitude = jax.random.uniform(split_keys[1], (BLOCKS, NORB), jnp.float32, 0.75, 1.0)
    jitter = jax.random.truncated_normal(split_keys[2], -3.0, 3.0, (BLOCKS, NORB, NORB), jnp.float32)
    return 4.0 * magnitude[:, :, None] * partner + jitter * (0.25 / math.sqrt(NORB))


def draw_sigma_prev(key, part):
    split_keys = jax.random.split(key)
    jitter = jax.random.truncated_normal(split_keys[0], -3.0, 3.0, (ENERGIES, BLOCKS, NORB, NORB), jnp.float32)
    jitter = jitter * (0.5 / math.sqrt(NORB))
    mirrored = jitter + jnp.swapaxes(jitter, 2, 3)
    diagonal = jax.random.uniform(split_keys[1], (ENERGIES, BLOCKS, NORB), jnp.float32, 0.0, 2.0)
    total = mirrored + diagonal[..., None] * jnp.eye(NORB, dtype=jnp.float32)
    return total.astype(jnp.bfloat16)


def draw_shifts(key, part):
    values = jax.random.randint(jax.random.fold_in(key, 3), (MODES,), 1, SMAX + 1)
    chosen = jax.random.randint(jax.random.fold_in(key, 7), (), 0, MODES)
    return jnp.where(jnp.arange(MODES) == chosen, SMAX, values).astype(jnp.int32)


def setup_inputs(seed: int = 0) -> dict:
    seeds = jax.random.split(jax.random.key(seed), 6)
    cell_blocks = draw_cell_blocks(jax.random.fold_in(seeds[5], 71), 0)
    coupling_blocks = draw_coupling_blocks(jax.random.fold_in(seeds[5], 71), 0)
    sigma_prev = draw_sigma_prev(jax.random.fold_in(seeds[5], 71), 0)
    shifts = draw_shifts(jax.random.fold_in(seeds[5], 71), 0)
    strengths = jnp.clip(jnp.exp(jax.random.uniform(seeds[4], (MODES,), jnp.float32, math.log(0.5), math.log(2.0))), 0.5, 2.0)
    return dict(cell_blocks=cell_blocks, coupling_blocks=coupling_blocks, sigma_prev=sigma_prev, shifts=shifts, strengths=strengths)


highest = lax.Precision.HIGHEST
energy_span = 3.0

def product(left_matrix, right_matrix):
    return jnp.matmul(left_matrix, right_matrix, precision=highest)

def invert(matrix):
    factor = jnp.linalg.cholesky(matrix)
    identity = jnp.eye(matrix.shape[-1], dtype=matrix.dtype)
    return jax.scipy.linalg.cho_solve((factor, True), identity)

def symmetric(matrix):
    return 0.5 * (matrix + matrix.T)

def solve_chain(matrices, couplings):

    def advance(carried, members):
        matrix, coupling = members
        schur_block = matrix - product(coupling.T, product(carried, coupling))
        inverse = invert(schur_block)
        return (inverse, inverse)
    final_inverse, inverses = lax.scan(advance, invert(matrices[0]), (matrices, couplings))

    def retreat(carried, members):
        inverse, coupling = members
        green_block = symmetric(inverse + product(product(inverse, carried), inverse))
        return (product(product(coupling, green_block), coupling.T), green_block)
    final_fold, greens = lax.scan(retreat, jnp.zeros_like(matrices[0]), (inverses, couplings), reverse=True)
    return greens

def reference(cell_blocks, coupling_blocks, sigma_prev, shifts, strengths):
    batch_size = math.gcd(ENERGIES, 8)
    levels = energy_span * jnp.arange(ENERGIES).astype(jnp.float32) / ENERGIES
    identity = jnp.eye(NORB, dtype=jnp.float32)

    def one_energy(level, previous):
        matrices = cell_blocks + level * identity + previous.astype(jnp.float32)
        return solve_chain(matrices, coupling_blocks)

    def one_batch(members):
        return jax.vmap(one_energy)(members[0], members[1])
    greens = lax.map(one_batch, (levels.reshape(ENERGIES // batch_size, batch_size), sigma_prev.reshape(ENERGIES // batch_size, batch_size, BLOCKS, NORB, NORB)))
    greens = greens.reshape(ENERGIES, BLOCKS, NORB, NORB)
    padded = jnp.pad(greens, ((SMAX, SMAX), (0, 0), (0, 0), (0, 0)))
    spread = jnp.zeros_like(greens)
    for phonon in range(MODES):
        below_rows = lax.dynamic_slice_in_dim(padded, SMAX - shifts[phonon], ENERGIES, 0)
        above_rows = lax.dynamic_slice_in_dim(padded, SMAX + shifts[phonon], ENERGIES, 0)
        spread = spread + strengths[phonon] * (below_rows + above_rows)
    return spread
```

```python
import functools

import jax
import jax.numpy as jnp
from jax import lax
from jax.experimental import pallas as pl
from jax.experimental.pallas import tpu as pltpu
from jax.sharding import PartitionSpec as P

MODES = 4
LEVEL_STEP = 3.0 / 384.0
RESIDUAL_MAX = 1e-3

f32 = jnp.float32
bf16 = jnp.bfloat16


def parts_of(matrix):
    high = matrix.astype(bf16)
    return high, (matrix - high.astype(f32)).astype(bf16)


def product_1(left, right):
    return jnp.dot(left, right, preferred_element_type=f32)


def product_3(left, right):
    return product_1(left[0], right[0]) + (
        product_1(left[1], right[0]) + product_1(left[0], right[1])
    )


def product_full(left, right):
    return jnp.dot(left, right, preferred_element_type=f32, precision=lax.Precision.HIGHEST)


def diagonal_mask(size):
    rows = lax.broadcasted_iota(jnp.int32, (size, size), 0)
    columns = lax.broadcasted_iota(jnp.int32, (size, size), 1)
    return rows == columns


def invert_series(matrix, diagonal):
    size = matrix.shape[0]
    mass = jnp.sum(jnp.where(diagonal, matrix, 0.0), axis=0, keepdims=True)
    scale = size / jnp.sum(mass, axis=1, keepdims=True)
    one = jnp.where(diagonal, 1.0, 0.0).astype(f32)
    rest = one - matrix * scale
    rest_parts = parts_of(rest)
    rest_2 = product_1(rest_parts[0], rest_parts[0])
    rest_2b = rest_2.astype(bf16)
    rest_3 = product_1(rest_parts[0], rest_2b)
    rest_4 = product_1(rest_2b, rest_2b)
    tail = rest + rest_2 + rest_3
    tail = tail + rest_4 + product_1(tail.astype(bf16), rest_4.astype(bf16))
    tail_parts = parts_of(tail)
    residual = rest - tail + product_3(rest_parts, tail_parts)
    tail = tail + residual + product_1(tail_parts[0], residual.astype(bf16))
    squared = jnp.sum(jnp.sum(residual * residual, axis=0, keepdims=True), axis=1, keepdims=True)
    return scale * (one + tail), squared


def invert_direct(matrix, diagonal, work):
    size = matrix.shape[0]
    rows = lax.broadcasted_iota(jnp.int32, (size, size), 0)
    columns = lax.broadcasted_iota(jnp.int32, (size, size), 1)
    work[...] = matrix

    def eliminate(pivot, _):
        values = work[...]
        row = work[pl.ds(pivot, 1), :]
        on_row, on_column = (rows == pivot, columns == pivot)
        column = jnp.sum(jnp.where(on_column, values, 0.0), axis=1, keepdims=True)
        corner = jnp.sum(jnp.where(on_column[:1], row, 0.0), axis=1, keepdims=True)
        scaled = row / corner
        updated = jnp.where(on_column, -column / corner, values - column * scaled)
        pivot_row = jnp.where(on_column[:1], 1.0 / corner, scaled)
        work[...] = jnp.where(on_row, pivot_row, updated)
        return 0

    lax.fori_loop(0, size, eliminate, 0)
    inverse = work[...]
    one = jnp.where(diagonal, 1.0, 0.0).astype(f32)
    return inverse + product_full(inverse, one - product_full(matrix, inverse))


def symmetric(matrix):
    return 0.5 * (matrix + matrix.T)


def eliminate_kernel(
    cell_ref, coupling_ref, sigma_ref, sum_ref, first_ref, fold_ref, second_ref, far_ref, work
):
    part = lax.axis_index("space")
    position = lax.axis_index("energy") * lax.axis_size("elem") + lax.axis_index("elem")
    level = position.astype(f32) * LEVEL_STEP
    near = part == 0
    size = cell_ref.shape[-1]
    diagonal = diagonal_mask(size)

    def block(index):
        return cell_ref[index] + jnp.where(diagonal, level, 0.0) + sigma_ref[0, index].astype(f32)

    def chain(invert, product, parts):
        outer, inner, last = (block(part), block(0), block(1))
        link = coupling_ref[part]
        link_turned = link.T
        link, link_turned = (
            jnp.where(near, link, link_turned), jnp.where(near, link_turned, link)
        )
        inner_link = coupling_ref[1 - part]
        inner_turned = inner_link.T
        inner_link, inner_turned = (
            jnp.where(near, inner_link, inner_turned), jnp.where(near, inner_turned, inner_link)
        )
        first, error = invert(outer)
        fold = product(parts(first), parts(link))
        second, error_second = invert(inner - product(parts(link_turned), parts(fold)))
        far = product(parts(second), parts(inner_link))
        total = jnp.where(near, last, 0.0) - product(parts(inner_turned), parts(far))
        first_ref[...] = first
        fold_ref[...] = fold
        second_ref[...] = second
        far_ref[...] = far
        sum_ref[...] = total
        return jnp.maximum(error, error_second)

    error = chain(lambda m: invert_series(m, diagonal), product_3, parts_of)

    @pl.when(jnp.logical_not(error[0, 0] <= RESIDUAL_MAX))
    def _():
        chain(
            lambda m: (invert_direct(m, diagonal, work), jnp.zeros((1, 1), f32)),
            product_full,
            lambda m: m,
        )


def recover_kernel(own_ref, other_ref, first_ref, fold_ref, second_ref, far_ref, green_ref, work):
    near = lax.axis_index("space") == 0
    size = own_ref.shape[-1]
    diagonal = diagonal_mask(size)
    groups, _, rows, _ = green_ref.shape

    def chain(invert, product, parts):
        middle, error = invert(own_ref[...] + other_ref[...])
        middle = symmetric(middle)
        far = far_ref[...]
        second = symmetric(
            second_ref[...] + product(parts(product(parts(far), parts(middle))), parts(far.T))
        )
        green_ref[:, 0] = second.reshape(groups, rows, size)

        @pl.when(near)
        def _():
            green_ref[:, 1] = middle.reshape(groups, rows, size)

        @pl.when(jnp.logical_not(near))
        def _():
            fold = fold_ref[...]
            outer = symmetric(
                first_ref[...] + product(parts(product(parts(fold), parts(second))), parts(fold.T))
            )
            green_ref[:, 1] = outer.reshape(groups, rows, size)

        return error

    error = chain(lambda m: invert_series(m, diagonal), product_3, parts_of)

    @pl.when(jnp.logical_not(error[0, 0] <= RESIDUAL_MAX))
    def _():
        chain(
            lambda m: (invert_direct(m, diagonal, work), jnp.zeros((1, 1), f32)),
            product_full,
            lambda m: m,
        )


def spread_kernel(shifts_ref, strengths_ref, below_ref, own_ref, above_ref, out_ref, rim, sems):
    width = own_ref.shape[0]
    copies = [
        pltpu.make_async_copy(source, rim.at[pl.ds(place * width, width)], sems.at[place])
        for place, source in enumerate((below_ref, own_ref, above_ref))
    ]
    for copy in copies:
        copy.start()
    for copy in copies:
        copy.wait()

    def one(index, _):
        total = None
        for phonon in range(MODES):
            shift = shifts_ref[phonon]
            term = strengths_ref[phonon] * (rim[width + index - shift] + rim[width + index + shift])
            total = term if total is None else total + term
        out_ref[index] = total
        return 0

    lax.fori_loop(0, width, one, 0, unroll=4)


def body(cell_blocks, coupling_blocks, sigma_prev, shifts, strengths):
    orbitals = sigma_prev.shape[2]
    elem_size = lax.axis_size("elem")
    square = jax.ShapeDtypeStruct((orbitals, orbitals), f32)
    vmem = pl.BlockSpec(memory_space=pltpu.VMEM)
    smem = pl.BlockSpec(memory_space=pltpu.SMEM)
    anywhere = pl.BlockSpec(memory_space=pl.ANY)
    own, first, fold, second, far = pl.pallas_call(
        eliminate_kernel,
        out_shape=[square] * 5,
        in_specs=[vmem] * 3,
        out_specs=[vmem] * 5,
        scratch_shapes=[pltpu.VMEM((orbitals, orbitals), f32)],
    )(cell_blocks, coupling_blocks, sigma_prev)
    other = lax.ppermute(own, "space", [(0, 1), (1, 0)])
    green = pl.pallas_call(
        recover_kernel,
        out_shape=jax.ShapeDtypeStruct((elem_size, 2, orbitals // elem_size, orbitals), f32),
        in_specs=[vmem] * 6,
        out_specs=vmem,
        scratch_shapes=[pltpu.VMEM((orbitals, orbitals), f32)],
    )(own, other, first, fold, second, far)
    arrived = lax.all_to_all(green, "elem", split_axis=0, concat_axis=0, tiled=True)
    ends = lax.axis_size("energy") - 1
    below = lax.ppermute(arrived, "energy", [(i, i + 1) for i in range(ends)])
    above = lax.ppermute(arrived, "energy", [(i + 1, i) for i in range(ends)])
    width = arrived.shape[0]
    return pl.pallas_call(
        spread_kernel,
        out_shape=jax.ShapeDtypeStruct(arrived.shape, f32),
        in_specs=[smem, smem, anywhere, anywhere, anywhere],
        out_specs=vmem,
        scratch_shapes=[
            pltpu.VMEM((3 * width,) + arrived.shape[1:], f32),
            pltpu.SemaphoreType.DMA((3,)),
        ],
    )(shifts, strengths, below, arrived, above)


def solution(mesh):
    in_specs = (
        P("space", None, None),
        P("space", None, None),
        P(("energy", "elem"), "space", None, None),
        P(),
        P(),
    )
    out_specs = P("energy", "space", "elem", None)
    return jax.shard_map(body, mesh=mesh, in_specs=in_specs, out_specs=out_specs, check_vma=False)
```

```python
import functools

import jax
import jax.numpy as jnp
from jax import lax
from jax.experimental import pallas as pl
from jax.experimental.pallas import tpu as pltpu
from jax.sharding import PartitionSpec as P

MODES = 4
STEPS = 4
LEVEL_STEP = 3.0 / 384.0
RESIDUAL_MAX = 1e-3
VMEM_BYTES = 12 * 1024 * 1024

f32 = jnp.float32
bf16 = jnp.bfloat16


def parts_of(matrix):
    high = matrix.astype(bf16)
    return high, (matrix - high.astype(f32)).astype(bf16)


def product_1(left, right):
    half = left.shape[0] // 2
    return jnp.concatenate(
        [
            jnp.dot(rows, right, preferred_element_type=f32)
            for rows in (left[:half], left[half:])
        ],
        axis=0,
    )


def product_3(left, right):
    return product_1(left[0], right[0]) + (
        product_1(left[1], right[0]) + product_1(left[0], right[1])
    )


def product_full(left, right):
    return jnp.dot(left, right, preferred_element_type=f32, precision=lax.Precision.HIGHEST)


def diagonal_mask(size):
    rows = lax.broadcasted_iota(jnp.int32, (size, size), 0)
    columns = lax.broadcasted_iota(jnp.int32, (size, size), 1)
    return rows == columns


def invert_series(matrix, diagonal, started=None):
    size = matrix.shape[0]
    mass = jnp.sum(jnp.where(diagonal, matrix, 0.0), axis=0, keepdims=True)
    scale = size / jnp.sum(mass, axis=1, keepdims=True)
    one = jnp.where(diagonal, 1.0, 0.0).astype(f32)
    rest = one - matrix * scale
    rest_parts = parts_of(rest)
    if started is not None:
        started()
    rest_2 = product_1(rest_parts[0], rest_parts[0])
    rest_2b = rest_2.astype(bf16)
    rest_3 = product_1(rest_parts[0], rest_2b)
    rest_4 = product_1(rest_2b, rest_2b)
    tail = rest + rest_2 + rest_3
    tail = tail + rest_4 + product_1(tail.astype(bf16), rest_4.astype(bf16))
    tail_parts = parts_of(tail)
    residual = rest - tail + product_3(rest_parts, tail_parts)
    tail = tail + residual + product_1(tail_parts[0], residual.astype(bf16))
    squared = jnp.sum(jnp.sum(residual * residual, axis=0, keepdims=True), axis=1, keepdims=True)
    return scale * (one + tail), squared


def invert_direct(matrix, diagonal, work):
    size = matrix.shape[0]
    rows = lax.broadcasted_iota(jnp.int32, (size, size), 0)
    columns = lax.broadcasted_iota(jnp.int32, (size, size), 1)
    work[...] = matrix

    def eliminate(pivot, _):
        values = work[...]
        row = work[pl.ds(pivot, 1), :]
        on_row, on_column = (rows == pivot, columns == pivot)
        column = jnp.sum(jnp.where(on_column, values, 0.0), axis=1, keepdims=True)
        corner = jnp.sum(jnp.where(on_column[:1], row, 0.0), axis=1, keepdims=True)
        scaled = row / corner
        updated = jnp.where(on_column, -column / corner, values - column * scaled)
        pivot_row = jnp.where(on_column[:1], 1.0 / corner, scaled)
        work[...] = jnp.where(on_row, pivot_row, updated)
        return 0

    lax.fori_loop(0, size, eliminate, 0)
    inverse = work[...]
    one = jnp.where(diagonal, 1.0, 0.0).astype(f32)
    return inverse + product_full(inverse, one - product_full(matrix, inverse))


def symmetric(matrix):
    return 0.5 * (matrix + matrix.T)


def eliminate_kernel(
    cell_hbm,
    coupling_hbm,
    sigma_hbm,
    sum_ref,
    first_ref,
    fold_ref,
    second_ref,
    far_ref,
    cell_ref,
    coupling_ref,
    sigma_ref,
    work,
    sems,
):
    part = lax.axis_index("space")
    copies = [
        pltpu.make_async_copy(source.at[index], target.at[index], sems.at[number])
        for number, (source, target, index) in enumerate(
            (
                (cell_hbm, cell_ref, part),
                (sigma_hbm.at[0], sigma_ref, part),
                (coupling_hbm, coupling_ref, part),
                (cell_hbm, cell_ref, 1 - part),
                (sigma_hbm.at[0], sigma_ref, 1 - part),
                (coupling_hbm, coupling_ref, 1 - part),
            )
        )
    ]
    for copy in copies:
        copy.start()
    position = lax.axis_index("energy") * lax.axis_size("elem") + lax.axis_index("elem")
    level = position.astype(f32) * LEVEL_STEP
    near = part == 0
    size = cell_ref.shape[-1]
    diagonal = diagonal_mask(size)

    def block(index):
        return cell_ref[index] + jnp.where(diagonal, level, 0.0) + sigma_ref[index].astype(f32)

    def arrive():
        for copy in copies[2:]:
            copy.wait()

    def chain(invert_outer, invert, product, parts):
        first, error = invert_outer(block(part))
        inner, last = (block(0), block(1))
        link = coupling_ref[part]
        link_turned = link.T
        link, link_turned = (
            jnp.where(near, link, link_turned), jnp.where(near, link_turned, link)
        )
        inner_link = coupling_ref[1 - part]
        inner_turned = inner_link.T
        inner_link, inner_turned = (
            jnp.where(near, inner_link, inner_turned), jnp.where(near, inner_turned, inner_link)
        )
        fold = product(parts(first), parts(link))
        second, error_second = invert(inner - product(parts(link_turned), parts(fold)))
        far = product(parts(second), parts(inner_link))
        total = jnp.where(near, last, 0.0) - product(parts(inner_turned), parts(far))
        first_ref[...] = first
        fold_ref[...] = fold
        second_ref[...] = second
        far_ref[...] = far
        sum_ref[...] = total
        return jnp.maximum(error, error_second)

    for copy in copies[:2]:
        copy.wait()
    error = chain(
        lambda m: invert_series(m, diagonal, arrive),
        lambda m: invert_series(m, diagonal),
        product_3,
        parts_of,
    )

    @pl.when(jnp.logical_not(error[0, 0] <= RESIDUAL_MAX))
    def _():
        direct = lambda m: (invert_direct(m, diagonal, work), jnp.zeros((1, 1), f32))
        chain(direct, direct, product_full, lambda m: m)


def recover_kernel(own_ref, other_ref, first_ref, fold_ref, second_ref, far_ref, green_ref, work):
    near = lax.axis_index("space") == 0
    size = own_ref.shape[-1]
    diagonal = diagonal_mask(size)
    groups, _, rows, _ = green_ref.shape

    def chain(invert, product, parts):
        middle, error = invert(own_ref[...] + other_ref[...])
        middle = symmetric(middle)
        far = far_ref[...]
        second = symmetric(
            second_ref[...] + product(parts(product(parts(far), parts(middle))), parts(far.T))
        )
        green_ref[:, 0] = second.reshape(groups, rows, size)

        @pl.when(near)
        def _():
            green_ref[:, 1] = middle.reshape(groups, rows, size)

        @pl.when(jnp.logical_not(near))
        def _():
            fold = fold_ref[...]
            outer = symmetric(
                first_ref[...] + product(parts(product(parts(fold), parts(second))), parts(fold.T))
            )
            green_ref[:, 1] = outer.reshape(groups, rows, size)

        return error

    error = chain(lambda m: invert_series(m, diagonal), product_3, parts_of)

    @pl.when(jnp.logical_not(error[0, 0] <= RESIDUAL_MAX))
    def _():
        chain(
            lambda m: (invert_direct(m, diagonal, work), jnp.zeros((1, 1), f32)),
            product_full,
            lambda m: m,
        )


def inner_kernel(shifts_ref, strengths_ref, own_ref, out_ref):
    width = own_ref.shape[0]

    def one(index, _):
        total = None
        for phonon in range(MODES):
            low, high = (index - shifts_ref[phonon], index + shifts_ref[phonon])
            strength = strengths_ref[phonon]
            term = jnp.where(low >= 0, strength, 0.0) * own_ref[jnp.maximum(low, 0)]
            term += jnp.where(high < width, strength, 0.0) * own_ref[jnp.minimum(high, width - 1)]
            total = term if total is None else total + term
        out_ref[index] = total
        return 0

    lax.fori_loop(0, width, one, 0, unroll=4)


def outer_kernel(shifts_ref, strengths_ref, inner_ref, below_ref, above_ref, out_ref):
    width = below_ref.shape[0]
    span = out_ref.shape[0]
    start = pl.program_id(0) * span

    def one(step, _):
        index = start + step
        total = inner_ref[step]
        for phonon in range(MODES):
            low, high = (index - shifts_ref[phonon], index + shifts_ref[phonon])
            strength = strengths_ref[phonon]
            total += (
                jnp.where(low < 0, strength, 0.0)
                * below_ref[jnp.minimum(low + width, width - 1)]
            )
            total += (
                jnp.where(high >= width, strength, 0.0) * above_ref[jnp.maximum(high - width, 0)]
            )
        out_ref[step] = total
        return 0

    lax.fori_loop(0, span, one, 0, unroll=4)


def body(cell_blocks, coupling_blocks, sigma_prev, shifts, strengths):
    orbitals = sigma_prev.shape[2]
    elem_size = lax.axis_size("elem")
    square = jax.ShapeDtypeStruct((orbitals, orbitals), f32)
    vmem = pl.BlockSpec(memory_space=pltpu.VMEM)
    smem = pl.BlockSpec(memory_space=pltpu.SMEM)
    hbm = pl.BlockSpec(memory_space=pltpu.HBM)
    own, first, fold, second, far = pl.pallas_call(
        eliminate_kernel,
        out_shape=[square] * 5,
        in_specs=[hbm] * 3,
        out_specs=[vmem] * 5,
        scratch_shapes=[
            pltpu.VMEM(cell_blocks.shape, f32),
            pltpu.VMEM(coupling_blocks.shape, f32),
            pltpu.VMEM(sigma_prev.shape[1:], sigma_prev.dtype),
            pltpu.VMEM((orbitals, orbitals), f32),
            pltpu.SemaphoreType.DMA((6,)),
        ],
        compiler_params=pltpu.CompilerParams(vmem_limit_bytes=VMEM_BYTES),
    )(*(
        pltpu.with_memory_space_constraint(argument, pltpu.HBM)
        for argument in (cell_blocks, coupling_blocks, sigma_prev)
    ))
    other = lax.ppermute(own, "space", [(0, 1), (1, 0)])
    green = pl.pallas_call(
        recover_kernel,
        out_shape=jax.ShapeDtypeStruct((elem_size, 2, orbitals // elem_size, orbitals), f32),
        in_specs=[vmem] * 6,
        out_specs=vmem,
        scratch_shapes=[pltpu.VMEM((orbitals, orbitals), f32)],
        compiler_params=pltpu.CompilerParams(vmem_limit_bytes=VMEM_BYTES),
    )(own, other, first, fold, second, far)
    arrived = lax.all_to_all(green, "elem", split_axis=0, concat_axis=0, tiled=True)
    ends = lax.axis_size("energy") - 1
    below = lax.ppermute(arrived, "energy", [(i, i + 1) for i in range(ends)])
    above = lax.ppermute(arrived, "energy", [(i + 1, i) for i in range(ends)])
    limits = pltpu.CompilerParams(vmem_limit_bytes=VMEM_BYTES)
    inner = pl.pallas_call(
        inner_kernel,
        out_shape=jax.ShapeDtypeStruct(arrived.shape, f32),
        in_specs=[smem, smem, vmem],
        out_specs=vmem,
        compiler_params=limits,
        cost_estimate=pl.CostEstimate(
            flops=16 * arrived.size, bytes_accessed=8 * arrived.size, transcendentals=0
        ),
    )(shifts, strengths, arrived)
    piece = pl.BlockSpec((arrived.shape[0] // STEPS,) + arrived.shape[1:], lambda i: (i, 0, 0, 0))
    return pl.pallas_call(
        outer_kernel,
        grid=(STEPS,),
        out_shape=jax.ShapeDtypeStruct(arrived.shape, f32),
        in_specs=[smem, smem, piece, vmem, vmem],
        out_specs=piece,
        compiler_params=limits,
    )(shifts, strengths, inner, below, above)


def solution(mesh):
    in_specs = (
        P("space", None, None),
        P("space", None, None),
        P(("energy", "elem"), "space", None, None),
        P(),
        P(),
    )
    out_specs = P("energy", "space", "elem", None)
    return jax.shard_map(body, mesh=mesh, in_specs=in_specs, out_specs=out_specs, check_vma=False)
```

```python
import functools

import jax
import jax.numpy as jnp
from jax import lax
from jax.experimental import pallas as pl
from jax.experimental.pallas import tpu as pltpu
from jax.sharding import PartitionSpec as P

MODES = 4
STEPS = 2
LEVEL_STEP = 3.0 / 384.0
RESIDUAL_MAX = 1e-3
VMEM_BYTES = 12 * 1024 * 1024

f32 = jnp.float32
bf16 = jnp.bfloat16


def parts_of(matrix):
    high = matrix.astype(bf16)
    return high, (matrix - high.astype(f32)).astype(bf16)


def product_1(left, right):
    half = left.shape[0] // 2
    return jnp.concatenate(
        [
            jnp.dot(rows, right, preferred_element_type=f32)
            for rows in (left[:half], left[half:])
        ],
        axis=0,
    )


def product_3(left, right):
    half = left[0].shape[0] // 2
    results = []
    for rows in (slice(0, half), slice(half, None)):
        both = jnp.dot(
            jnp.concatenate([left[0][rows], left[1][rows]], axis=0),
            right[0],
            preferred_element_type=f32,
        )
        results.append(
            both[:half] + (both[half:] + jnp.dot(left[0][rows], right[1], preferred_element_type=f32))
        )
    return jnp.concatenate(results, axis=0)


def product_full(left, right):
    return jnp.dot(left, right, preferred_element_type=f32, precision=lax.Precision.HIGHEST)


def diagonal_mask(size):
    rows = lax.broadcasted_iota(jnp.int32, (size, size), 0)
    columns = lax.broadcasted_iota(jnp.int32, (size, size), 1)
    return rows == columns


def invert_series(matrix, diagonal, started=None):
    size = matrix.shape[0]
    mass = jnp.sum(jnp.where(diagonal, matrix, 0.0), axis=0, keepdims=True)
    scale = size / jnp.sum(mass, axis=1, keepdims=True)
    one = jnp.where(diagonal, 1.0, 0.0).astype(f32)
    rest = one - matrix * scale
    rest_parts = parts_of(rest)
    if started is not None:
        started()
    rest_2 = product_1(rest_parts[0], rest_parts[0])
    rest_2b = rest_2.astype(bf16)
    rest_3 = product_1(rest_parts[0], rest_2b)
    rest_4 = product_1(rest_2b, rest_2b)
    tail = rest + rest_2 + rest_3
    tail = tail + rest_4 + product_1(tail.astype(bf16), rest_4.astype(bf16))
    tail_parts = parts_of(tail)
    residual = rest - tail + product_3(rest_parts, tail_parts)
    tail = tail + residual + product_1(tail_parts[0], residual.astype(bf16))
    squared = jnp.sum(jnp.sum(residual * residual, axis=0, keepdims=True), axis=1, keepdims=True)
    return scale * (one + tail), squared


def invert_direct(matrix, diagonal, work):
    size = matrix.shape[0]
    rows = lax.broadcasted_iota(jnp.int32, (size, size), 0)
    columns = lax.broadcasted_iota(jnp.int32, (size, size), 1)
    work[...] = matrix

    def eliminate(pivot, _):
        values = work[...]
        row = work[pl.ds(pivot, 1), :]
        on_row, on_column = (rows == pivot, columns == pivot)
        column = jnp.sum(jnp.where(on_column, values, 0.0), axis=1, keepdims=True)
        corner = jnp.sum(jnp.where(on_column[:1], row, 0.0), axis=1, keepdims=True)
        scaled = row / corner
        updated = jnp.where(on_column, -column / corner, values - column * scaled)
        pivot_row = jnp.where(on_column[:1], 1.0 / corner, scaled)
        work[...] = jnp.where(on_row, pivot_row, updated)
        return 0

    lax.fori_loop(0, size, eliminate, 0)
    inverse = work[...]
    one = jnp.where(diagonal, 1.0, 0.0).astype(f32)
    return inverse + product_full(inverse, one - product_full(matrix, inverse))


def symmetric(matrix):
    return 0.5 * (matrix + matrix.T)


def eliminate_kernel(
    cell_hbm,
    coupling_hbm,
    sigma_hbm,
    sum_ref,
    first_ref,
    fold_ref,
    second_ref,
    far_ref,
    cell_ref,
    coupling_ref,
    sigma_ref,
    work,
    sems,
):
    part = lax.axis_index("space")
    copies = [
        pltpu.make_async_copy(source.at[index], target.at[index], sems.at[number])
        for number, (source, target, index) in enumerate(
            (
                (cell_hbm, cell_ref, part),
                (sigma_hbm.at[0], sigma_ref, part),
                (coupling_hbm, coupling_ref, part),
                (cell_hbm, cell_ref, 1 - part),
                (sigma_hbm.at[0], sigma_ref, 1 - part),
                (coupling_hbm, coupling_ref, 1 - part),
            )
        )
    ]
    for copy in copies:
        copy.start()
    position = lax.axis_index("energy") * lax.axis_size("elem") + lax.axis_index("elem")
    level = position.astype(f32) * LEVEL_STEP
    near = part == 0
    size = cell_ref.shape[-1]
    diagonal = diagonal_mask(size)

    def block(index):
        return cell_ref[index] + jnp.where(diagonal, level, 0.0) + sigma_ref[index].astype(f32)

    def arrive():
        for copy in copies[2:]:
            copy.wait()

    def chain(invert_outer, invert, product, parts):
        first, error = invert_outer(block(part))
        inner, last = (block(0), block(1))
        link = coupling_ref[part]
        link_turned = link.T
        link, link_turned = (
            jnp.where(near, link, link_turned), jnp.where(near, link_turned, link)
        )
        inner_link = coupling_ref[1 - part]
        inner_turned = inner_link.T
        inner_link, inner_turned = (
            jnp.where(near, inner_link, inner_turned), jnp.where(near, inner_turned, inner_link)
        )
        fold = product(parts(first), parts(link))
        second, error_second = invert(inner - product(parts(link_turned), parts(fold)))
        far = product(parts(second), parts(inner_link))
        total = jnp.where(near, last, 0.0) - product(parts(inner_turned), parts(far))
        first_ref[...] = first
        fold_ref[...] = fold
        second_ref[...] = second
        far_ref[...] = far
        sum_ref[...] = total
        return jnp.maximum(error, error_second)

    for copy in copies[:2]:
        copy.wait()
    error = chain(
        lambda m: invert_series(m, diagonal, arrive),
        lambda m: invert_series(m, diagonal),
        product_3,
        parts_of,
    )

    @pl.when(jnp.logical_not(error[0, 0] <= RESIDUAL_MAX))
    def _():
        direct = lambda m: (invert_direct(m, diagonal, work), jnp.zeros((1, 1), f32))
        chain(direct, direct, product_full, lambda m: m)


def recover_kernel(own_ref, other_ref, first_ref, fold_ref, second_ref, far_ref, green_ref, work):
    near = lax.axis_index("space") == 0
    size = own_ref.shape[-1]
    diagonal = diagonal_mask(size)
    groups, _, rows, _ = green_ref.shape

    def chain(invert, product, parts):
        middle, error = invert(own_ref[...] + other_ref[...])
        middle = symmetric(middle)
        far = far_ref[...]
        second = symmetric(
            second_ref[...] + product(parts(product(parts(far), parts(middle))), parts(far.T))
        )
        green_ref[:, 0] = second.reshape(groups, rows, size)

        @pl.when(near)
        def _():
            green_ref[:, 1] = middle.reshape(groups, rows, size)

        @pl.when(jnp.logical_not(near))
        def _():
            fold = fold_ref[...]
            outer = symmetric(
                first_ref[...] + product(parts(product(parts(fold), parts(second))), parts(fold.T))
            )
            green_ref[:, 1] = outer.reshape(groups, rows, size)

        return error

    error = chain(lambda m: invert_series(m, diagonal), product_3, parts_of)

    @pl.when(jnp.logical_not(error[0, 0] <= RESIDUAL_MAX))
    def _():
        chain(
            lambda m: (invert_direct(m, diagonal, work), jnp.zeros((1, 1), f32)),
            product_full,
            lambda m: m,
        )


def spread_kernel(
    shifts_ref, strengths_ref, below_ref, own_ref, above_ref, out_hbm, rim, out_ref, sems
):
    width = own_ref.shape[0]
    span = width // STEPS
    for place, source in enumerate((below_ref, own_ref, above_ref)):
        rim[place * width : (place + 1) * width] = source[...]
    shifts = [shifts_ref[phonon] for phonon in range(MODES)]
    strengths = [strengths_ref[phonon] for phonon in range(MODES)]
    copies = []
    for step in range(STEPS):
        for index in range(step * span, (step + 1) * span):
            total = None
            for shift, strength in zip(shifts, strengths):
                term = strength * (rim[width + index - shift] + rim[width + index + shift])
                total = term if total is None else total + term
            out_ref[index] = total
        piece = pl.ds(step * span, span)
        copies.append(pltpu.make_async_copy(out_ref.at[piece], out_hbm.at[piece], sems.at[step]))
        copies[-1].start()
    for copy in copies:
        copy.wait()


def body(cell_blocks, coupling_blocks, sigma_prev, shifts, strengths):
    orbitals = sigma_prev.shape[2]
    elem_size = lax.axis_size("elem")
    square = jax.ShapeDtypeStruct((orbitals, orbitals), f32)
    vmem = pl.BlockSpec(memory_space=pltpu.VMEM)
    smem = pl.BlockSpec(memory_space=pltpu.SMEM)
    hbm = pl.BlockSpec(memory_space=pltpu.HBM)
    own, first, fold, second, far = pl.pallas_call(
        eliminate_kernel,
        out_shape=[square] * 5,
        in_specs=[hbm] * 3,
        out_specs=[vmem] * 5,
        scratch_shapes=[
            pltpu.VMEM(cell_blocks.shape, f32),
            pltpu.VMEM(coupling_blocks.shape, f32),
            pltpu.VMEM(sigma_prev.shape[1:], sigma_prev.dtype),
            pltpu.VMEM((orbitals, orbitals), f32),
            pltpu.SemaphoreType.DMA((6,)),
        ],
        compiler_params=pltpu.CompilerParams(vmem_limit_bytes=VMEM_BYTES),
    )(*(
        pltpu.with_memory_space_constraint(argument, pltpu.HBM)
        for argument in (cell_blocks, coupling_blocks, sigma_prev)
    ))
    other = lax.ppermute(own, "space", [(0, 1), (1, 0)])
    green = pl.pallas_call(
        recover_kernel,
        out_shape=jax.ShapeDtypeStruct((elem_size, 2, orbitals // elem_size, orbitals), f32),
        in_specs=[vmem] * 6,
        out_specs=vmem,
        scratch_shapes=[pltpu.VMEM((orbitals, orbitals), f32)],
        compiler_params=pltpu.CompilerParams(vmem_limit_bytes=VMEM_BYTES),
    )(own, other, first, fold, second, far)
    arrived = lax.all_to_all(green, "elem", split_axis=0, concat_axis=0, tiled=True)
    ends = lax.axis_size("energy") - 1
    below = lax.ppermute(arrived, "energy", [(i, i + 1) for i in range(ends)])
    above = lax.ppermute(arrived, "energy", [(i + 1, i) for i in range(ends)])
    width = arrived.shape[0]
    return pl.pallas_call(
        spread_kernel,
        out_shape=jax.ShapeDtypeStruct(arrived.shape, f32),
        in_specs=[smem, smem, vmem, vmem, vmem],
        out_specs=hbm,
        scratch_shapes=[
            pltpu.VMEM((3 * width,) + arrived.shape[1:], f32),
            pltpu.VMEM(arrived.shape, f32),
            pltpu.SemaphoreType.DMA((STEPS,)),
        ],
        compiler_params=pltpu.CompilerParams(vmem_limit_bytes=VMEM_BYTES),
    )(shifts, strengths, below, arrived, above)


def solution(mesh):
    in_specs = (
        P("space", None, None),
        P("space", None, None),
        P(("energy", "elem"), "space", None, None),
        P(),
        P(),
    )
    out_specs = P("energy", "space", "elem", None)
    return jax.shard_map(body, mesh=mesh, in_specs=in_specs, out_specs=out_specs, check_vma=False)
```

```python
import jax
import jax.numpy as jnp
from jax import lax
from jax.experimental import pallas as pl
from jax.experimental.pallas import tpu as pltpu
from jax.sharding import PartitionSpec as P

MODES = 4
STEPS = 4
PIECES = 2
LEVEL_STEP = 3.0 / 384.0
RESIDUAL_MAX = 1e-3
VMEM_BYTES = 12 * 1024 * 1024

f32 = jnp.float32
bf16 = jnp.bfloat16


def parts_of(matrix):
    high = matrix.astype(bf16)
    return high, (matrix - high.astype(f32)).astype(bf16)


def product_0(left, right):
    return jnp.dot(left, right, preferred_element_type=f32)


def product_1(left, right):
    half = left.shape[0] // 2
    return jnp.concatenate(
        [
            jnp.dot(rows, right, preferred_element_type=f32)
            for rows in (left[:half], left[half:])
        ],
        axis=0,
    )


def product_3(left, right):
    half = left[0].shape[0] // 2
    results = []
    for rows in (slice(0, half), slice(half, None)):
        both = jnp.dot(
            jnp.concatenate([left[0][rows], left[1][rows]], axis=0),
            right[0],
            preferred_element_type=f32,
        )
        results.append(
            both[:half] + (both[half:] + jnp.dot(left[0][rows], right[1], preferred_element_type=f32))
        )
    return jnp.concatenate(results, axis=0)


def product_full(left, right):
    return jnp.dot(left, right, preferred_element_type=f32, precision=lax.Precision.HIGHEST)


def diagonal_mask(size):
    rows = lax.broadcasted_iota(jnp.int32, (size, size), 0)
    columns = lax.broadcasted_iota(jnp.int32, (size, size), 1)
    return rows == columns


def invert_series(matrix, diagonal, started=None):
    size = matrix.shape[0]
    mass = jnp.sum(jnp.where(diagonal, matrix, 0.0), axis=0, keepdims=True)
    scale = size / jnp.sum(mass, axis=1, keepdims=True)
    one = jnp.where(diagonal, 1.0, 0.0).astype(f32)
    rest = one - matrix * scale
    rest_parts = parts_of(rest)
    if started is not None:
        started()
    rest_2 = product_1(rest_parts[0], rest_parts[0])
    rest_2b = rest_2.astype(bf16)
    half = size // 2
    rows = rest_parts[0]
    pair = [
        product_0(jnp.concatenate([rows[a:b], rest_2b[a:b]], axis=0), rest_2b)
        for a, b in ((0, half), (half, size))
    ]
    rest_3 = jnp.concatenate([pair[0][:half], pair[1][:half]], axis=0)
    rest_4 = jnp.concatenate([pair[0][half:], pair[1][half:]], axis=0)
    tail = rest + rest_2 + rest_3
    tail = tail + rest_4 + product_1(tail.astype(bf16), rest_4.astype(bf16))
    tail_parts = parts_of(tail)
    residual = rest - tail + product_3(rest_parts, tail_parts)
    tail = tail + residual + product_1(tail_parts[0], residual.astype(bf16))
    squared = jnp.sum(jnp.sum(residual * residual, axis=0, keepdims=True), axis=1, keepdims=True)
    return scale * (one + tail), squared


def invert_direct(matrix, diagonal, work):
    size = matrix.shape[0]
    rows = lax.broadcasted_iota(jnp.int32, (size, size), 0)
    columns = lax.broadcasted_iota(jnp.int32, (size, size), 1)
    work[...] = matrix

    def eliminate(pivot, _):
        values = work[...]
        row = work[pl.ds(pivot, 1), :]
        on_row, on_column = (rows == pivot, columns == pivot)
        column = jnp.sum(jnp.where(on_column, values, 0.0), axis=1, keepdims=True)
        corner = jnp.sum(jnp.where(on_column[:1], row, 0.0), axis=1, keepdims=True)
        scaled = row / corner
        updated = jnp.where(on_column, -column / corner, values - column * scaled)
        pivot_row = jnp.where(on_column[:1], 1.0 / corner, scaled)
        work[...] = jnp.where(on_row, pivot_row, updated)
        return 0

    lax.fori_loop(0, size, eliminate, 0)
    inverse = work[...]
    one = jnp.where(diagonal, 1.0, 0.0).astype(f32)
    return inverse + product_full(inverse, one - product_full(matrix, inverse))


def symmetric(matrix):
    return 0.5 * (matrix + matrix.T)


def eliminate_kernel(
    cell_hbm,
    coupling_hbm,
    sigma_hbm,
    sum_ref,
    first_ref,
    fold_ref,
    second_ref,
    far_ref,
    cell_ref,
    coupling_ref,
    sigma_ref,
    work,
    sems,
):
    part = lax.axis_index("space")
    near = part == 0
    copies = []

    def bring(source, target, index, pieces=1):
        height = target.shape[1] // pieces
        for piece in range(pieces):
            rows = pl.ds(piece * height, height)
            copies.append(
                pltpu.make_async_copy(
                    source.at[index, rows], target.at[index, rows], sems.at[len(copies)]
                )
            )
            copies[-1].start()

    bring(cell_hbm, cell_ref, part, PIECES)
    bring(sigma_hbm.at[0], sigma_ref, part)
    first_copies = len(copies)
    bring(coupling_hbm, coupling_ref, part)
    bring(cell_hbm, cell_ref, 1 - part)
    bring(sigma_hbm.at[0], sigma_ref, 1 - part)
    bring(coupling_hbm, coupling_ref, 1 - part)
    position = lax.axis_index("energy") * lax.axis_size("elem") + lax.axis_index("elem")
    level = position.astype(f32) * LEVEL_STEP
    size = cell_ref.shape[-1]
    diagonal = diagonal_mask(size)

    def block(index):
        return cell_ref[index] + jnp.where(diagonal, level, 0.0) + sigma_ref[index].astype(f32)

    def arrive():
        for copy in copies[first_copies:]:
            copy.wait()

    def chain(invert_outer, invert, product, parts):
        first, error = invert_outer(block(part))
        inner, last = (block(0), block(1))
        link = coupling_ref[part]
        link_turned = link.T
        link, link_turned = (
            jnp.where(near, link, link_turned), jnp.where(near, link_turned, link)
        )
        inner_link = coupling_ref[1 - part]
        inner_turned = inner_link.T
        inner_link, inner_turned = (
            jnp.where(near, inner_link, inner_turned), jnp.where(near, inner_turned, inner_link)
        )
        fold = product(parts(first), parts(link))
        second, error_second = invert(inner - product(parts(link_turned), parts(fold)))
        far = product(parts(second), parts(inner_link))
        total = jnp.where(near, last, 0.0) - product(parts(inner_turned), parts(far))
        first_ref[...] = first
        fold_ref[...] = fold
        second_ref[...] = second
        far_ref[...] = far
        sum_ref[...] = total
        return jnp.maximum(error, error_second)

    for copy in copies[:first_copies]:
        copy.wait()
    error = chain(
        lambda m: invert_series(m, diagonal, arrive),
        lambda m: invert_series(m, diagonal),
        product_3,
        parts_of,
    )

    @pl.when(jnp.logical_not(error[0, 0] <= RESIDUAL_MAX))
    def _():
        direct = lambda m: (invert_direct(m, diagonal, work), jnp.zeros((1, 1), f32))
        chain(direct, direct, product_full, lambda m: m)


def recover_kernel(own_ref, other_ref, first_ref, fold_ref, second_ref, far_ref, green_ref, work):
    near = lax.axis_index("space") == 0
    size = own_ref.shape[-1]
    diagonal = diagonal_mask(size)
    groups, _, rows, _ = green_ref.shape

    def store(index, block):
        green_ref[:, index] = block.reshape(groups, rows, size)

    def chain(invert, product, parts):
        middle, error = invert(own_ref[...] + other_ref[...])
        far = far_ref[...]
        second = second_ref[...] + product(
            parts(product(parts(far), parts(middle))), parts(far.T)
        )
        middle = symmetric(middle)
        store(1, middle)
        store(0, symmetric(second))

        @pl.when(jnp.logical_not(near))
        def _():
            fold = fold_ref[...]
            outer = product(parts(product(parts(fold), parts(second))), parts(fold.T))
            store(1, symmetric(first_ref[...] + outer))

        return error

    error = chain(lambda m: invert_series(m, diagonal), product_3, parts_of)

    @pl.when(jnp.logical_not(error[0, 0] <= RESIDUAL_MAX))
    def _():
        chain(
            lambda m: (invert_direct(m, diagonal, work), jnp.zeros((1, 1), f32)),
            product_full,
            lambda m: m,
        )


def spread_kernel(
    shifts_ref, strengths_ref, below_ref, own_ref, above_ref, out_hbm, rim, out_ref, sems
):
    width = own_ref.shape[0]
    span = width // STEPS
    for place, source in enumerate((below_ref, own_ref, above_ref)):
        rim[place * width : (place + 1) * width] = source[...]
    shifts = [shifts_ref[phonon] for phonon in range(MODES)]
    strengths = [strengths_ref[phonon] for phonon in range(MODES)]
    copies = []
    for step in range(STEPS):
        for index in range(step * span, (step + 1) * span):
            total = None
            for shift, strength in zip(shifts, strengths):
                term = strength * (rim[width + index - shift] + rim[width + index + shift])
                total = term if total is None else total + term
            out_ref[index] = total
        piece = pl.ds(step * span, span)
        copies.append(pltpu.make_async_copy(out_ref.at[piece], out_hbm.at[piece], sems.at[step]))
        copies[-1].start()
    for copy in copies:
        copy.wait()


def body(cell_blocks, coupling_blocks, sigma_prev, shifts, strengths):
    orbitals = sigma_prev.shape[2]
    elem_size = lax.axis_size("elem")
    square = jax.ShapeDtypeStruct((orbitals, orbitals), f32)
    vmem = pl.BlockSpec(memory_space=pltpu.VMEM)
    smem = pl.BlockSpec(memory_space=pltpu.SMEM)
    hbm = pl.BlockSpec(memory_space=pltpu.HBM)
    own, first, fold, second, far = pl.pallas_call(
        eliminate_kernel,
        out_shape=[square] * 5,
        in_specs=[hbm] * 3,
        out_specs=[vmem] * 5,
        scratch_shapes=[
            pltpu.VMEM(cell_blocks.shape, f32),
            pltpu.VMEM(coupling_blocks.shape, f32),
            pltpu.VMEM(sigma_prev.shape[1:], sigma_prev.dtype),
            pltpu.VMEM((orbitals, orbitals), f32),
            pltpu.SemaphoreType.DMA((5 + PIECES,)),
        ],
        compiler_params=pltpu.CompilerParams(
            vmem_limit_bytes=VMEM_BYTES
        ),
    )(*(
        pltpu.with_memory_space_constraint(argument, pltpu.HBM)
        for argument in (cell_blocks, coupling_blocks, sigma_prev)
    ))
    other = lax.ppermute(own, "space", [(0, 1), (1, 0)])
    green = pl.pallas_call(
        recover_kernel,
        out_shape=jax.ShapeDtypeStruct((elem_size, 2, orbitals // elem_size, orbitals), f32),
        in_specs=[vmem] * 6,
        out_specs=vmem,
        scratch_shapes=[pltpu.VMEM((orbitals, orbitals), f32)],
        compiler_params=pltpu.CompilerParams(vmem_limit_bytes=VMEM_BYTES),
    )(own, other, first, fold, second, far)
    arrived = lax.all_to_all(green, "elem", split_axis=0, concat_axis=0, tiled=True)
    ends = lax.axis_size("energy") - 1
    below = lax.ppermute(arrived, "energy", [(i, i + 1) for i in range(ends)])
    above = lax.ppermute(arrived, "energy", [(i + 1, i) for i in range(ends)])
    width = arrived.shape[0]
    return pl.pallas_call(
        spread_kernel,
        out_shape=jax.ShapeDtypeStruct(arrived.shape, f32),
        in_specs=[smem, smem, vmem, vmem, vmem],
        out_specs=hbm,
        scratch_shapes=[
            pltpu.VMEM((3 * width,) + arrived.shape[1:], f32),
            pltpu.VMEM(arrived.shape, f32),
            pltpu.SemaphoreType.DMA((STEPS,)),
        ],
        compiler_params=pltpu.CompilerParams(vmem_limit_bytes=VMEM_BYTES),
    )(shifts, strengths, below, arrived, above)


def solution(mesh):
    in_specs = (
        P("space", None, None),
        P("space", None, None),
        P(("energy", "elem"), "space", None, None),
        P(),
        P(),
    )
    out_specs = P("energy", "space", "elem", None)
    return jax.shard_map(body, mesh=mesh, in_specs=in_specs, out_specs=out_specs, check_vma=False)
```

```python
import jax
import jax.numpy as jnp
from jax import lax
from jax.experimental import pallas as pl
from jax.experimental.pallas import tpu as pltpu
from jax.sharding import PartitionSpec as P

MODES = 4
STEPS = 4
PIECES = 2
STAGGER_NS = 3500
LEVEL_STEP = 3.0 / 384.0
RESIDUAL_MAX = 1e-3
VMEM_BYTES = 12 * 1024 * 1024

f32 = jnp.float32
bf16 = jnp.bfloat16


def parts_of(matrix):
    high = matrix.astype(bf16)
    return high, (matrix - high.astype(f32)).astype(bf16)


def product_0(left, right):
    return jnp.dot(left, right, preferred_element_type=f32)


def product_1(left, right):
    half = left.shape[0] // 2
    return jnp.concatenate(
        [
            jnp.dot(rows, right, preferred_element_type=f32)
            for rows in (left[:half], left[half:])
        ],
        axis=0,
    )


def product_3(left, right):
    half = left[0].shape[0] // 2
    results = []
    for rows in (slice(0, half), slice(half, None)):
        both = jnp.dot(
            jnp.concatenate([left[0][rows], left[1][rows]], axis=0),
            right[0],
            preferred_element_type=f32,
        )
        results.append(
            both[:half] + (both[half:] + jnp.dot(left[0][rows], right[1], preferred_element_type=f32))
        )
    return jnp.concatenate(results, axis=0)


def product_full(left, right):
    return jnp.dot(left, right, preferred_element_type=f32, precision=lax.Precision.HIGHEST)


def diagonal_mask(size):
    rows = lax.broadcasted_iota(jnp.int32, (size, size), 0)
    columns = lax.broadcasted_iota(jnp.int32, (size, size), 1)
    return rows == columns


def invert_series(matrix, diagonal, started=None):
    size = matrix.shape[0]
    mass = jnp.sum(jnp.where(diagonal, matrix, 0.0), axis=0, keepdims=True)
    scale = size / jnp.sum(mass, axis=1, keepdims=True)
    one = jnp.where(diagonal, 1.0, 0.0).astype(f32)
    rest = one - matrix * scale
    rest_parts = parts_of(rest)
    if started is not None:
        started()
    rest_2 = product_1(rest_parts[0], rest_parts[0])
    rest_2b = rest_2.astype(bf16)
    half = size // 2
    rows = rest_parts[0]
    pair = [
        product_0(jnp.concatenate([rows[a:b], rest_2b[a:b]], axis=0), rest_2b)
        for a, b in ((0, half), (half, size))
    ]
    rest_3 = jnp.concatenate([pair[0][:half], pair[1][:half]], axis=0)
    rest_4 = jnp.concatenate([pair[0][half:], pair[1][half:]], axis=0)
    tail = rest + rest_2 + rest_3
    tail = tail + rest_4 + product_1(tail.astype(bf16), rest_4.astype(bf16))
    tail_parts = parts_of(tail)
    residual = rest - tail + product_3(rest_parts, tail_parts)
    tail = tail + residual + product_1(tail_parts[0], residual.astype(bf16))
    squared = jnp.sum(jnp.sum(residual * residual, axis=0, keepdims=True), axis=1, keepdims=True)
    return scale * (one + tail), squared


def invert_direct(matrix, diagonal, work):
    size = matrix.shape[0]
    rows = lax.broadcasted_iota(jnp.int32, (size, size), 0)
    columns = lax.broadcasted_iota(jnp.int32, (size, size), 1)
    work[...] = matrix

    def eliminate(pivot, _):
        values = work[...]
        row = work[pl.ds(pivot, 1), :]
        on_row, on_column = (rows == pivot, columns == pivot)
        column = jnp.sum(jnp.where(on_column, values, 0.0), axis=1, keepdims=True)
        corner = jnp.sum(jnp.where(on_column[:1], row, 0.0), axis=1, keepdims=True)
        scaled = row / corner
        updated = jnp.where(on_column, -column / corner, values - column * scaled)
        pivot_row = jnp.where(on_column[:1], 1.0 / corner, scaled)
        work[...] = jnp.where(on_row, pivot_row, updated)
        return 0

    lax.fori_loop(0, size, eliminate, 0)
    inverse = work[...]
    one = jnp.where(diagonal, 1.0, 0.0).astype(f32)
    return inverse + product_full(inverse, one - product_full(matrix, inverse))


def symmetric(matrix):
    return 0.5 * (matrix + matrix.T)


def eliminate_kernel(
    cell_hbm,
    coupling_hbm,
    sigma_hbm,
    sum_ref,
    first_ref,
    fold_ref,
    second_ref,
    far_ref,
    cell_ref,
    coupling_ref,
    sigma_ref,
    work,
    sems,
):
    part = lax.axis_index("space")
    near = part == 0
    copies = []

    def bring(source, target, index, pieces=1):
        height = target.shape[1] // pieces
        for piece in range(pieces):
            rows = pl.ds(piece * height, height)
            copies.append(
                pltpu.make_async_copy(
                    source.at[index, rows], target.at[index, rows], sems.at[len(copies)]
                )
            )
            copies[-1].start()

    bring(cell_hbm, cell_ref, part, PIECES)
    bring(sigma_hbm.at[0], sigma_ref, part)
    first_copies = len(copies)
    bring(coupling_hbm, coupling_ref, part)
    bring(cell_hbm, cell_ref, 1 - part)
    bring(sigma_hbm.at[0], sigma_ref, 1 - part)
    bring(coupling_hbm, coupling_ref, 1 - part)
    position = lax.axis_index("energy") * lax.axis_size("elem") + lax.axis_index("elem")
    level = position.astype(f32) * LEVEL_STEP
    size = cell_ref.shape[-1]
    diagonal = diagonal_mask(size)

    def block(index):
        return cell_ref[index] + jnp.where(diagonal, level, 0.0) + sigma_ref[index].astype(f32)

    def arrive():
        for copy in copies[first_copies:]:
            copy.wait()

    def chain(invert_outer, invert, product, parts):
        first, error = invert_outer(block(part))
        inner, last = (block(0), block(1))
        link = coupling_ref[part]
        link_turned = link.T
        link, link_turned = (
            jnp.where(near, link, link_turned), jnp.where(near, link_turned, link)
        )
        inner_link = coupling_ref[1 - part]
        inner_turned = inner_link.T
        inner_link, inner_turned = (
            jnp.where(near, inner_link, inner_turned), jnp.where(near, inner_turned, inner_link)
        )
        fold = product(parts(first), parts(link))
        second, error_second = invert(inner - product(parts(link_turned), parts(fold)))
        far = product(parts(second), parts(inner_link))
        total = jnp.where(near, last, 0.0) - product(parts(inner_turned), parts(far))
        first_ref[...] = first
        fold_ref[...] = fold
        second_ref[...] = second
        far_ref[...] = far
        sum_ref[...] = total
        return jnp.maximum(error, error_second)

    for copy in copies[:first_copies]:
        copy.wait()
    error = chain(
        lambda m: invert_series(m, diagonal, arrive),
        lambda m: invert_series(m, diagonal),
        product_3,
        parts_of,
    )

    @pl.when(jnp.logical_not(error[0, 0] <= RESIDUAL_MAX))
    def _():
        direct = lambda m: (invert_direct(m, diagonal, work), jnp.zeros((1, 1), f32))
        chain(direct, direct, product_full, lambda m: m)


def recover_kernel(own_ref, other_ref, first_ref, fold_ref, second_ref, far_ref, green_ref, work):
    near = lax.axis_index("space") == 0
    size = own_ref.shape[-1]
    diagonal = diagonal_mask(size)
    groups, _, rows, _ = green_ref.shape

    def store(index, block):
        green_ref[:, index] = block.reshape(groups, rows, size)

    def chain(invert, product, parts):
        middle, error = invert(own_ref[...] + other_ref[...])
        far = far_ref[...]
        second = second_ref[...] + product(
            parts(product(parts(far), parts(middle))), parts(far.T)
        )
        middle = symmetric(middle)
        store(1, middle)
        store(0, symmetric(second))

        @pl.when(jnp.logical_not(near))
        def _():
            fold = fold_ref[...]
            outer = product(parts(product(parts(fold), parts(second))), parts(fold.T))
            store(1, symmetric(first_ref[...] + outer))

        return error

    error = chain(lambda m: invert_series(m, diagonal), product_3, parts_of)

    @pl.when(jnp.logical_not(error[0, 0] <= RESIDUAL_MAX))
    def _():
        chain(
            lambda m: (invert_direct(m, diagonal, work), jnp.zeros((1, 1), f32)),
            product_full,
            lambda m: m,
        )

    @pl.when(near)
    def _():
        pl.delay(STAGGER_NS)


def spread_kernel(
    shifts_ref, strengths_ref, below_ref, own_ref, above_ref, out_hbm, rim, out_ref, sems
):
    width = own_ref.shape[0]
    span = width // STEPS
    for place, source in enumerate((below_ref, own_ref, above_ref)):
        rim[place * width : (place + 1) * width] = source[...]
    shifts = [shifts_ref[phonon] for phonon in range(MODES)]
    strengths = [strengths_ref[phonon] for phonon in range(MODES)]
    copies = []
    for step in range(STEPS):
        for index in range(step * span, (step + 1) * span):
            total = None
            for shift, strength in zip(shifts, strengths):
                term = strength * (rim[width + index - shift] + rim[width + index + shift])
                total = term if total is None else total + term
            out_ref[index] = total
        piece = pl.ds(step * span, span)
        copies.append(pltpu.make_async_copy(out_ref.at[piece], out_hbm.at[piece], sems.at[step]))
        copies[-1].start()
    for copy in copies:
        copy.wait()


def body(cell_blocks, coupling_blocks, sigma_prev, shifts, strengths):
    orbitals = sigma_prev.shape[2]
    elem_size = lax.axis_size("elem")
    square = jax.ShapeDtypeStruct((orbitals, orbitals), f32)
    vmem = pl.BlockSpec(memory_space=pltpu.VMEM)
    smem = pl.BlockSpec(memory_space=pltpu.SMEM)
    hbm = pl.BlockSpec(memory_space=pltpu.HBM)
    own, first, fold, second, far = pl.pallas_call(
        eliminate_kernel,
        out_shape=[square] * 5,
        in_specs=[hbm] * 3,
        out_specs=[vmem] * 5,
        scratch_shapes=[
            pltpu.VMEM(cell_blocks.shape, f32),
            pltpu.VMEM(coupling_blocks.shape, f32),
            pltpu.VMEM(sigma_prev.shape[1:], sigma_prev.dtype),
            pltpu.VMEM((orbitals, orbitals), f32),
            pltpu.SemaphoreType.DMA((5 + PIECES,)),
        ],
        compiler_params=pltpu.CompilerParams(vmem_limit_bytes=VMEM_BYTES),
    )(*(
        pltpu.with_memory_space_constraint(argument, pltpu.HBM)
        for argument in (cell_blocks, coupling_blocks, sigma_prev)
    ))
    other = lax.ppermute(own, "space", [(0, 1), (1, 0)])
    green = pl.pallas_call(
        recover_kernel,
        out_shape=jax.ShapeDtypeStruct((elem_size, 2, orbitals // elem_size, orbitals), f32),
        in_specs=[vmem] * 6,
        out_specs=vmem,
        scratch_shapes=[pltpu.VMEM((orbitals, orbitals), f32)],
        compiler_params=pltpu.CompilerParams(vmem_limit_bytes=VMEM_BYTES),
    )(own, other, first, fold, second, far)
    arrived = lax.all_to_all(green, "elem", split_axis=0, concat_axis=0, tiled=True)
    ends = lax.axis_size("energy") - 1
    below = lax.ppermute(arrived, "energy", [(i, i + 1) for i in range(ends)])
    above = lax.ppermute(arrived, "energy", [(i + 1, i) for i in range(ends)])
    width = arrived.shape[0]
    return pl.pallas_call(
        spread_kernel,
        out_shape=jax.ShapeDtypeStruct(arrived.shape, f32),
        in_specs=[smem, smem, vmem, vmem, vmem],
        out_specs=hbm,
        scratch_shapes=[
            pltpu.VMEM((3 * width,) + arrived.shape[1:], f32),
            pltpu.VMEM(arrived.shape, f32),
            pltpu.SemaphoreType.DMA((STEPS,)),
        ],
        compiler_params=pltpu.CompilerParams(vmem_limit_bytes=VMEM_BYTES),
    )(shifts, strengths, below, arrived, above)


def solution(mesh):
    in_specs = (
        P("space", None, None),
        P("space", None, None),
        P(("energy", "elem"), "space", None, None),
        P(),
        P(),
    )
    out_specs = P("energy", "space", "elem", None)
    return jax.shard_map(body, mesh=mesh, in_specs=in_specs, out_specs=out_specs, check_vma=False)
```
